128 devices in a mesh: section: 4 (over x), vocab: 2 (over core), dp: 16 (over z, y).
Axes of the slice: x: 4, y: 4, z: 4, core: 2. Of those that a mesh axis runs over, the one named last changes fastest.
Arguments:
- entering: bfloat16 [8, 16, 32, 2048], P(None, 'dp', 'vocab'), may hold values from -6 to 6
- depths: int32 [8], replicated, may hold values from 1 to 4
- targets: int32 [8, 16, 32], P(None, 'dp'), may hold values from 0 to 64127
- norm_gain: float32 [4, 2048], P('section'), may hold values from 0.5 to 1.5
- w_gate: bfloat16 [4, 2048, 7168], P('section', 'dp', 'vocab'), may hold values from -0.125 to 0.125
- w_up: bfloat16 [4, 2048, 7168], P('section', 'dp', 'vocab'), may hold values from -0.125 to 0.125
- w_down: bfloat16 [4, 7168, 2048], P('section', 'vocab', 'dp'), may hold values from -0.0625 to 0.0625
- final_gain: float32 [2048], replicated, may hold values from 0.5 to 1.5
- head_weight: bfloat16 [2048, 64128], P(None, ('section', 'vocab')), may hold values from -32 to 32
Outputs:
- token_loss: float32 [8, 16, 32], P(None, 'dp')
- mean_loss: float32 [], replicated
The draws below stay inside these ranges and needn't reach their ends.
All inputs are finite; a program needn't handle non-finite values.
Results may differ from the reference program's by a relative error of at most 0.0055.
Values may be sent and summed in bfloat16 or wider, within the bound.
A program may use at most 192 MiB of HBM per device.

```python
import math
import jax
import jax.numpy as jnp
import numpy as np
from jax import lax

D = 2048
FF = 7168
VOCAB = 64128
MICRO = 8
LAYERS = 4
POS = 32
REPLICAS = 16


def draw_head_weight(key, part):
    key_base = jax.random.fold_in(key, 11)
    column_pos = jnp.arange(VOCAB, dtype=jnp.float32)
    spread = 2.7 + 0.5 * column_pos / VOCAB
    result = jax.random.normal(key_base, (D, VOCAB), jnp.float32) * spread[None, :] / math.sqrt(D)
    result = jnp.clip(result, -32.0, 32.0)
    return result.astype(jnp.bfloat16)


def place_ends(values, rng, smallest, top_value):
    longest = values.shape.index(max(values.shape))
    spots = []
    for shift in (0, 1):
        where = [jax.random.randint(jax.random.fold_in(rng, axis), (), 0, length) for axis, length in enumerate(values.shape)]
        where[longest] = (where[longest] + shift) % values.shape[longest]
        spots.append(tuple(where))
    return values.at[spots[0]].set(smallest).at[spots[1]].set(top_value)


def shard_levels(stream_key, extent, cuts, least, top_value):
    def one(dim, parts):
        steps = jax.random.uniform(jax.random.fold_in(jax.random.fold_in(stream_key, 6), dim), (parts,), jnp.float32, least / len(cuts), top_value / len(cuts))
        return jnp.repeat(jnp.exp(steps), extent[dim] // parts).reshape((-1,) + (1,) * (len(extent) - dim - 1))

    level = one(*cuts[0])
    for cut in cuts[1:]:
        level = level * one(*cut)
    return level


def rank_bounds(amount, slope):
    weights = [(1 << 20) // math.isqrt(standing ** slope) + 1 for standing in range(1, amount + 1)]
    deviation = 1 + sum(weights) // (1 << 30)
    return np.cumsum(np.array([max(1, weight // deviation) for weight in weights]))


def ranked(own_key, dims, count, lean):
    grid = rank_bounds(count, lean)
    ticket = jax.random.randint(jax.random.fold_in(own_key, 1), dims, 0, int(grid[count - 1]))
    standing = jnp.searchsorted(jnp.asarray(grid, jnp.int32), ticket, side="right")
    return jax.random.permutation(jax.random.fold_in(own_key, 2), count)[standing].astype(jnp.int32)


def scatter_about(own_key, shape, deviation, most, shards=(), held_as=jnp.bfloat16):
    level = shard_levels(own_key, shape, shards, -0.22, 0.18) if shards else 1.0
    values = jax.random.normal(own_key, shape, jnp.float32) * deviation * level
    return jnp.minimum(jnp.maximum(values, -most), most).astype(held_as)


def setup_inputs(seed: int = 0) -> dict:
    key_of = jax.random.split(jax.random.key(seed), 10)
    entering = scatter_about(key_of[0], (MICRO, REPLICAS, POS, D), 1.0, 6.0, ((1, 16), (2, 2)))
    depths = place_ends(jax.random.randint(key_of[1], (MICRO,), 1, LAYERS + 1), jax.random.fold_in(key_of[1], 1), 1, LAYERS).astype(jnp.int32)
    targets = place_ends(ranked(key_of[2], (MICRO, REPLICAS, POS), VOCAB, 2), jax.random.fold_in(key_of[2], 3), 0, VOCAB - 1).astype(jnp.int32)
    norm_gain = jnp.clip(1.0 + 0.1 * jax.random.normal(key_of[3], (LAYERS, D), jnp.float32), 0.5, 1.5)
    w_gate = scatter_about(key_of[4], (LAYERS, D, FF), D ** -0.5, 0.125, ((0, 4), (1, 16), (2, 2)))
    w_up = scatter_about(key_of[5], (LAYERS, D, FF), D ** -0.5, 0.125, ((0, 4), (1, 16), (2, 2)))
    w_down = scatter_about(key_of[6], (LAYERS, FF, D), FF ** -0.5, 0.0625, ((0, 4), (1, 2), (2, 16)))
    final_gain = jnp.clip(1.0 + 0.1 * jax.random.normal(key_of[7], (D,), jnp.float32), 0.5, 1.5)
    head_weight = draw_head_weight(jax.random.fold_in(key_of[9], 71), 0)
    return dict(entering=entering, depths=depths, targets=targets, norm_gain=norm_gain, w_gate=w_gate, w_up=w_up, w_down=w_down, final_gain=final_gain, head_weight=head_weight)


EPS = 1e-05

def rms_scaled(values, gain):
    widened = values.astype(jnp.float32)
    return widened * lax.rsqrt(lax.optimization_barrier(jnp.mean(widened * widened, axis=-1, keepdims=True)) + EPS) * gain

def reference(entering, depths, targets, norm_gain, w_gate, w_up, w_down, final_gain, head_weight):
    micro_count = entering.shape[0]
    width = entering.shape[3]
    current = entering.reshape(micro_count, -1, width)
    labels = targets.reshape(micro_count, -1)

    def run_layer(carried, layer_args):
        gain, gate_matrix, up_matrix, down_matrix, layer_index = layer_args
        normed = rms_scaled(carried, gain).astype(jnp.bfloat16).reshape(-1, width)
        gate_part = jnp.dot(normed, gate_matrix, preferred_element_type=jnp.float32)
        up_part = jnp.dot(normed, up_matrix, preferred_element_type=jnp.float32)
        hidden = (jax.nn.silu(gate_part) * up_part).astype(jnp.bfloat16)
        branch = jnp.dot(hidden, down_matrix, preferred_element_type=jnp.float32).reshape(carried.shape)
        moved = (carried.astype(jnp.float32) + branch).astype(jnp.bfloat16)
        active = (layer_index < depths)[:, None, None]
        return (jnp.where(active, moved, carried), None)
    layer_ids = jnp.arange(LAYERS, dtype=jnp.int32)
    current, unused = lax.scan(run_layer, current, (norm_gain, w_gate, w_up, w_down, layer_ids))
    finals = rms_scaled(current, final_gain).astype(jnp.bfloat16)

    def one_batch(batch_args):
        rows_now, labels_now = batch_args
        logits = jnp.dot(rows_now, head_weight, preferred_element_type=jnp.float32)
        peak = lax.optimization_barrier(jnp.max(logits, axis=-1, keepdims=True))
        spread_sum = jnp.log(lax.optimization_barrier(jnp.sum(jnp.exp(logits - peak), axis=-1))) + peak[:, 0]
        picked = jnp.take_along_axis(logits, labels_now[:, None].astype(jnp.int32), axis=1)[:, 0]
        return spread_sum - picked
    losses = lax.map(one_batch, (finals, labels))
    token_loss = losses.reshape(targets.shape)
    return (token_loss, jnp.mean(losses))
```

```python
import functools

import jax
import jax.numpy as jnp
from jax import lax
from jax.experimental import pallas as pl
from jax.experimental.pallas import tpu as pltpu
from jax.sharding import PartitionSpec as P

EPS = 1e-05
MESH = pl.DeviceIdType.MESH
SIDE = 4


def rms_scaled(values, gain):
    widened = values.astype(jnp.float32)
    return widened * lax.rsqrt(jnp.mean(widened * widened, axis=-1, keepdims=True) + EPS) * gain


def place():
    s, v, i = lax.axis_index("section"), lax.axis_index("vocab"), lax.axis_index("dp")
    z, y = lax.div(i, SIDE), lax.rem(i, SIDE)
    return s, v, i, y + v * (z - y), z + v * (y - z)


def dp_of(v, a, b):
    return SIDE * b + a + v * (SIDE - 1) * (a - b)


def turned(x, d):
    return lax.rem(x + d, SIDE)


def layers_kernel(
    ent_ref, act_ref, gain_ref, fgain_ref, wg_ref, wu_ref, wd_ref, fin_ref,
    wgu, wdn, gat, part, arr, xin, xout, hid,
    own_sem, w_send, w_recv, ag_send, ag_recv, rs_send, rs_recv, x_send, x_recv, f_send, f_recv,
):
    s, v, i, a, b = place()
    micro, half, width = ent_ref.shape
    hb = hid.shape[1]
    fr = wg_ref.shape[0]
    w_other = 1 - v
    last = SIDE - 1

    def to(src, dst, send, recv, where):
        return pltpu.make_async_remote_copy(
            src_ref=src, dst_ref=dst, send_sem=send, recv_sem=recv, device_id=where, device_id_type=MESH
        )

    barrier = pltpu.get_barrier_semaphore()
    for w in (0, 1):
        for d in range(1, SIDE):
            pl.semaphore_signal(barrier, inc=1, device_id=(s, w, dp_of(v, turned(a, d), b)), device_id_type=MESH)
            pl.semaphore_signal(barrier, inc=1, device_id=(s, w, dp_of(v, a, turned(b, d))), device_id_type=MESH)
            pl.semaphore_signal(barrier, inc=1, device_id=(turned(s, d), w, i), device_id_type=MESH)
    pl.semaphore_signal(barrier, inc=1, device_id=(s, w_other, i), device_id_type=MESH)
    pl.semaphore_wait(barrier, 6 * last + 1)

    def landing(k):
        rows = pl.ds(pl.multiple_of(k * fr, fr), fr)
        return wgu.at[rows, pl.ds(0, hb)], wgu.at[rows, pl.ds(hb, hb)], wdn.at[:, rows]

    def held(k):
        units = pl.ds(pl.multiple_of(k * hb, hb), hb)
        return wg_ref.at[:, units], wu_ref.at[:, units], wd_ref.at[units, :]

    def three(sources, k, send, recv, where):
        for src, dst in zip(sources, landing(k)):
            to(src, dst, send, recv, where).start()

    three_bytes = wgu.at[pl.ds(0, 3 * fr), pl.ds(0, hb)]

    def await_block(j, d):
        sem = w_recv.at[turned(a, j) * SIDE + turned(b, d)]
        pltpu.make_async_copy(three_bytes, three_bytes, sem).wait()

    right = (s, v, dp_of(v, a, turned(b, 1)))
    left = (s, v, dp_of(v, a, turned(b, last)))

    def pass_round(j, sources):
        k = dp_of(v, turned(a, j), b)
        recv = w_recv.at[turned(a, j) * SIDE + b]
        three(sources, k, w_send.at[3 + 2 * j], recv, right)
        three(sources, k, w_send.at[4 + 2 * j], recv, left)

    for src, dst in zip(held(a), landing(i)):
        pltpu.make_async_copy(src, dst, own_sem).start()
    for d in range(1, SIDE):
        peer = turned(a, d)
        three(held(peer), i, w_send.at[d - 1], w_recv.at[a * SIDE + b], (s, v, dp_of(v, peer, b)))
    pass_round(0, held(a))

    def to_group(src, block_own, block_other, send, recv):
        for d in range(1, SIDE):
            to(src, gat.at[block_own], send, recv, (s, v, dp_of(v, turned(a, d), b))).start()
        for d in range(SIDE):
            to(src, gat.at[block_other], send, recv, (s, w_other, dp_of(v, a, turned(b, d)))).start()

    def enter(m):
        @pl.when(s == 0)
        def _():
            xin[m] = ent_ref[m]

        @pl.when(s > 0)
        def _():
            pltpu.make_async_copy(xin.at[m], xin.at[m], x_recv.at[m]).wait()

        mine = m * 8 + a * 2 + v
        gat[mine] = rms_scaled(xin[m], gain_ref[...]).astype(jnp.bfloat16)
        to_group(gat.at[mine], mine, m * 8 + b * 2 + v, ag_send.at[m], ag_recv.at[m])

    def branch(m):
        seven = gat.at[pl.ds(0, 7)]
        pltpu.make_async_copy(seven, seven, ag_recv.at[m]).wait()
        rows = gat[pl.ds(pl.multiple_of(m * 8, 8), 8)].reshape(8 * half, width)
        both = jnp.dot(rows, wgu[...], preferred_element_type=jnp.float32)
        gate, up = both[:, :hb], both[:, hb:]
        hid[...] = (gate / (1.0 + jnp.exp(-gate)) * up).astype(jnp.bfloat16)
        out = jnp.dot(hid[...], wdn[...], preferred_element_type=jnp.float32)
        part[pl.ds(pl.multiple_of(m * 8, 8), 8)] = out.astype(jnp.bfloat16).reshape(8, half, width)
        slot = m * 8 + v * SIDE + a
        for d in range(1, SIDE):
            c = turned(a, d)
            for w in (0, 1):
                to(part.at[m * 8 + c * 2 + w], arr.at[slot], rs_send.at[m], rs_recv.at[m],
                   (s, w, dp_of(v, c, b))).start()
        to(part.at[m * 8 + a * 2 + w_other], arr.at[slot], rs_send.at[m], rs_recv.at[m], (s, w_other, i)).start()
        arr[slot] = part[m * 8 + a * 2 + v]

    def leave(m):
        seven = arr.at[pl.ds(0, 7)]
        pltpu.make_async_copy(seven, seven, rs_recv.at[m]).wait()
        total = arr[m * 8].astype(jnp.float32)
        for k in range(1, 8):
            total = total + arr[m * 8 + k].astype(jnp.float32)
        state = xin[m].astype(jnp.float32)
        state = jnp.where(act_ref[m] > 0.0, state + total, state).astype(jnp.bfloat16)

        @pl.when(s < last)
        def _():
            xout[m] = state
            to(xout.at[m], xin.at[m], x_send.at[m], x_recv.at[m], (s + 1, v, i)).start()

        @pl.when(s == last)
        def _():
            fin_ref[m * 2 + v] = rms_scaled(state, fgain_ref[...]).astype(jnp.bfloat16)
            mine = fin_ref.at[m * 2 + v]
            for d in range(1, SIDE):
                for w in (0, 1):
                    to(mine, mine, f_send.at[m], f_recv, (turned(s, d), w, i)).start()
            to(mine, mine, f_send.at[m], f_recv, (s, w_other, i)).start()

    enter(0)
    enter(1)

    for j in range(1, SIDE):
        await_block(j, 0)
        pass_round(j, landing(dp_of(v, turned(a, j), b)))
    for j in range(SIDE):
        d, where = (last, right) if j % 2 == 0 else (1, left)
        await_block(j, d)
        k = dp_of(v, turned(a, j), turned(b, d))
        three(landing(k), k, w_send.at[11 + j], w_recv.at[turned(a, j) * SIDE + turned(b, d)], where)
        await_block(j, SIDE - d)
    for j in range(SIDE):
        await_block(j, 2)
    pltpu.make_async_copy(three_bytes, three_bytes, own_sem).wait()

    def step(m, carry):
        branch(m)

        @pl.when(m > 0)
        def _():
            leave(m - 1)

        @pl.when(m + 2 < micro)
        def _():
            enter(m + 2)

        return carry

    lax.fori_loop(0, micro, step, 0)
    leave(micro - 1)

    @pl.when(s < last)
    def _():
        pltpu.make_async_copy(fin_ref, fin_ref, f_recv).wait()

    @pl.when(s == last)
    def _():
        others = fin_ref.at[pl.ds(0, micro)]
        pltpu.make_async_copy(others, others, f_recv).wait()

    for k in range(15):
        pltpu.make_async_copy(three_bytes, three_bytes, w_send.at[k]).wait()

    def drain(m, carry):
        seven, one = gat.at[pl.ds(0, 7)], xout.at[0]
        pltpu.make_async_copy(seven, seven, ag_send.at[m]).wait()
        pltpu.make_async_copy(seven, seven, rs_send.at[m]).wait()

        @pl.when(s < last)
        def _():
            pltpu.make_async_copy(one, one, x_send.at[m]).wait()

        @pl.when(s == last)
        def _():
            pltpu.make_async_copy(seven, seven, f_send.at[m]).wait()

        return carry

    lax.fori_loop(0, micro, drain, 0)


def through_layers(rows, active, gain, final_gain, w_gate, w_up, w_down):
    micro, half, width = rows.shape
    hb = w_gate.shape[1] // SIDE
    vmem, any_space = pl.BlockSpec(memory_space=pltpu.VMEM), pl.BlockSpec(memory_space=pl.ANY)
    dma = pltpu.SemaphoreType.DMA
    bf16 = jnp.bfloat16
    return pl.pallas_call(
        layers_kernel,
        out_shape=jax.ShapeDtypeStruct((2 * micro, half, width), bf16),
        in_specs=[vmem] * 4 + [any_space] * 3,
        out_specs=vmem,
        scratch_shapes=[
            pltpu.VMEM((width, 2 * hb), bf16),
            pltpu.VMEM((hb, width), bf16),
            pltpu.VMEM((micro * 8, half, width), bf16),
            pltpu.VMEM((micro * 8, half, width), bf16),
            pltpu.VMEM((micro * 8, half, width), bf16),
            pltpu.VMEM((micro, half, width), bf16),
            pltpu.VMEM((micro, half, width), bf16),
            pltpu.VMEM((8 * half, hb), bf16),
            dma(()), dma((15,)), dma((SIDE * SIDE,)),
            dma((micro,)), dma((micro,)), dma((micro,)), dma((micro,)),
            dma((micro,)), dma((micro,)), dma((micro,)), dma(()),
        ],
        compiler_params=pltpu.CompilerParams(
            collective_id=0, has_side_effects=True, vmem_limit_bytes=56 * 1024 * 1024
        ),
        name="layers",
    )(rows, active, gain, final_gain, w_gate, w_up, w_down)


def head_kernel(columns, fin_ref, head_ref, label_ref, out_ref, peak, total, picked):
    j = pl.program_id(0)
    rows, lanes = peak.shape
    tile = head_ref.shape[1]

    @pl.when(j == 0)
    def _():
        peak[...] = jnp.full_like(peak, -1e30)
        total[...] = jnp.zeros_like(total)
        picked[...] = jnp.zeros_like(picked)

    logits = jnp.dot(fin_ref[...], head_ref[...], preferred_element_type=jnp.float32)
    at = j * tile + lax.broadcasted_iota(jnp.int32, (rows, lanes), 1)
    groups = []
    for g in range(tile // lanes):
        groups.append(jnp.where(at + g * lanes < columns, logits[:, g * lanes : (g + 1) * lanes], -1e30))
    old = peak[...]
    new = old
    for values in groups:
        new = jnp.maximum(new, values)
    summed = total[...] * jnp.exp(old - new)
    found = picked[...]
    label = label_ref[...]
    for g, values in enumerate(groups):
        summed = summed + jnp.exp(values - new)
        found = found + jnp.where(at + g * lanes == label, values, 0.0)
    peak[...], total[...], picked[...] = new, summed, found

    @pl.when(j == pl.num_programs(0) - 1)
    def _():
        top = jnp.max(new, axis=1, keepdims=True)
        whole = jnp.sum(summed * jnp.exp(new - top), axis=1, keepdims=True)
        mine = jnp.sum(found, axis=1, keepdims=True)
        for k, column in enumerate((top, whole, mine)):
            out_ref[k : k + 1, :] = jnp.transpose(jnp.broadcast_to(column, (rows, lanes)))[0:1, :]
        out_ref[3:8, :] = jnp.zeros((5, rows), jnp.float32)


def head_sums(finals, head_weight, labels, tile=1024):
    rows, width = finals.shape
    columns = head_weight.shape[1]
    return pl.pallas_call(
        functools.partial(head_kernel, columns),
        out_shape=jax.ShapeDtypeStruct((8, rows), jnp.float32),
        grid=(pl.cdiv(columns, tile),),
        in_specs=[
            pl.BlockSpec((rows, width), lambda j: (0, 0)),
            pl.BlockSpec((width, tile), lambda j: (0, j)),
            pl.BlockSpec((rows, 128), lambda j: (0, 0)),
        ],
        out_specs=pl.BlockSpec((8, rows), lambda j: (0, 0)),
        scratch_shapes=[pltpu.VMEM((rows, 128), jnp.float32)] * 3,
        compiler_params=pltpu.CompilerParams(vmem_limit_bytes=40 * 1024 * 1024),
        name="head",
    )(finals, head_weight, labels)


def losses_kernel(count, sums_ref, loss_ref, mean_ref, shared, totals, own, s_send, s_recv, t_send, t_recv):
    s, v, i = lax.axis_index("section"), lax.axis_index("vocab"), lax.axis_index("dp")
    shards, shares = 8, totals.shape[0]
    barrier = pltpu.get_barrier_semaphore()
    me = s * 2 + v
    for d in range(1, shards):
        k = lax.rem(me + d, shards)
        pl.semaphore_signal(
            barrier, inc=1, device_id=(lax.div(k, 2), lax.rem(k, 2), i), device_id_type=MESH
        )
    for d in range(1, shares):
        pl.semaphore_signal(barrier, inc=1, device_id=(s, v, lax.rem(i + d, shares)), device_id_type=MESH)
    pl.semaphore_wait(barrier, shards + shares - 2)

    for d in range(1, shards):
        k = lax.rem(me + d, shards)
        pltpu.make_async_remote_copy(
            src_ref=sums_ref, dst_ref=shared.at[me], send_sem=s_send, recv_sem=s_recv,
            device_id=(lax.div(k, 2), lax.rem(k, 2), i), device_id_type=MESH,
        ).start()
    shared[me] = sums_ref[...]
    seven = shared.at[pl.ds(0, shards - 1)]
    pltpu.make_async_copy(seven, seven, s_recv).wait()
    everyone = shared[...]
    peaks = everyone[:, 0, :]
    peak = jnp.max(peaks, axis=0, keepdims=True)
    total = jnp.sum(everyone[:, 1, :] * jnp.exp(peaks - peak), axis=0, keepdims=True)
    picked = jnp.sum(everyone[:, 2, :], axis=0, keepdims=True)
    loss = jnp.log(total) + peak - picked
    loss_ref[...] = loss
    own[...] = jnp.broadcast_to(jnp.sum(loss, axis=1, keepdims=True), own.shape)
    for d in range(1, shares):
        pltpu.make_async_remote_copy(
            src_ref=own, dst_ref=totals.at[i], send_sem=t_send, recv_sem=t_recv,
            device_id=(s, v, lax.rem(i + d, shares)), device_id_type=MESH,
        ).start()
    totals[i] = own[...]
    rest = totals.at[pl.ds(0, shares - 1)]
    pltpu.make_async_copy(rest, rest, t_recv).wait()
    mean_ref[...] = jnp.sum(totals[...], axis=0) / count
    pltpu.make_async_copy(seven, seven, s_send).wait()
    pltpu.make_async_copy(rest, rest, t_send).wait()


def losses_of(sums, shares):
    rows = sums.shape[1]
    vmem = pl.BlockSpec(memory_space=pltpu.VMEM)
    dma = pltpu.SemaphoreType.DMA
    return pl.pallas_call(
        functools.partial(losses_kernel, float(rows * shares)),
        out_shape=(jax.ShapeDtypeStruct((1, rows), jnp.float32), jax.ShapeDtypeStruct((8, 128), jnp.float32)),
        in_specs=[vmem],
        out_specs=(vmem, vmem),
        scratch_shapes=[
            pltpu.VMEM((8, 8, rows), jnp.float32),
            pltpu.VMEM((shares, 8, 128), jnp.float32),
            pltpu.VMEM((8, 128), jnp.float32),
            dma(()), dma(()), dma(()), dma(()),
        ],
        compiler_params=pltpu.CompilerParams(collective_id=1, has_side_effects=True),
        name="losses",
    )(sums)


def on_device(entering, depths, targets, norm_gain, w_gate, w_up, w_down, final_gain, head_weight):
    s, v = lax.axis_index("section"), lax.axis_index("vocab")
    micro, _, half, width = entering.shape
    active = jnp.broadcast_to((s < depths).astype(jnp.float32)[:, None, None], (micro, 1, width))
    finals = through_layers(
        entering[:, 0], active, norm_gain, final_gain[None, :], w_gate[0], w_up[0], w_down[0]
    )
    rows = micro * 2 * half
    columns = head_weight.shape[1]
    labels = targets.reshape(rows, 1) - (s * 2 + v) * columns
    labels = jnp.where(labels < columns, labels, -1)
    sums = head_sums(finals.reshape(rows, width), head_weight, jnp.broadcast_to(labels, (rows, 128)))
    loss, mean = losses_of(sums, lax.axis_size("dp"))
    return loss.reshape(targets.shape), mean[0, 0]


def solution(mesh):
    in_specs = (
        P(None, "dp", "vocab", None),
        P(),
        P(None, "dp", None),
        P("section", None),
        P("section", "dp", "vocab"),
        P("section", "dp", "vocab"),
        P("section", "vocab", "dp"),
        P(),
        P(None, ("section", "vocab")),
    )
    out_specs = (P(None, "dp", None), P())
    return jax.shard_map(
        on_device, mesh=mesh, in_specs=in_specs, out_specs=out_specs, check_vma=False
    )
```

```python
import functools

import jax
import jax.numpy as jnp
from jax import lax
from jax.experimental import pallas as pl
from jax.experimental.pallas import tpu as pltpu
from jax.sharding import PartitionSpec as P

EPS = 1e-05
MESH = pl.DeviceIdType.MESH
SIDE = 4


def rms_scaled(values, gain):
    widened = values.astype(jnp.float32)
    return widened * lax.rsqrt(jnp.mean(widened * widened, axis=-1, keepdims=True) + EPS) * gain


def place():
    s, v, i = lax.axis_index("section"), lax.axis_index("vocab"), lax.axis_index("dp")
    z, y = lax.div(i, SIDE), lax.rem(i, SIDE)
    return s, v, i, y + v * (z - y), z + v * (y - z)


def dp_of(v, a, b):
    return SIDE * b + a + v * (SIDE - 1) * (a - b)


def turned(x, d):
    return lax.rem(x + d, SIDE)


def layers_kernel(
    ent_ref, act_ref, gain_ref, fgain_ref, wg_ref, wu_ref, wd_ref, fin_ref,
    wgu, wdn, gat, part, arr, xin, xout, hid,
    own_sem, w_send, w_recv, ag_send, ag_recv, rs_send, rs_recv, x_send, x_recv, f_send, f_recv,
):
    s, v, i, a, b = place()
    micro, half, width = ent_ref.shape
    hb = hid.shape[1]
    fr = wg_ref.shape[0]
    w_other = 1 - v
    last = SIDE - 1

    def to(src, dst, send, recv, where):
        return pltpu.make_async_remote_copy(
            src_ref=src, dst_ref=dst, send_sem=send, recv_sem=recv, device_id=where, device_id_type=MESH
        )

    barrier = pltpu.get_barrier_semaphore()
    for w in (0, 1):
        for d in range(1, SIDE):
            pl.semaphore_signal(barrier, inc=1, device_id=(s, w, dp_of(v, turned(a, d), b)), device_id_type=MESH)
            pl.semaphore_signal(barrier, inc=1, device_id=(s, w, dp_of(v, a, turned(b, d))), device_id_type=MESH)
            pl.semaphore_signal(barrier, inc=1, device_id=(turned(s, d), w, i), device_id_type=MESH)
    pl.semaphore_signal(barrier, inc=1, device_id=(s, w_other, i), device_id_type=MESH)
    pl.semaphore_wait(barrier, 6 * last + 1)

    def landing(k):
        rows = pl.ds(pl.multiple_of(k * fr, fr), fr)
        return wgu.at[rows, pl.ds(0, hb)], wgu.at[rows, pl.ds(hb, hb)], wdn.at[:, rows]

    def held(k):
        units = pl.ds(pl.multiple_of(k * hb, hb), hb)
        return wg_ref.at[:, units], wu_ref.at[:, units], wd_ref.at[units, :]

    def three(sources, k, send, recv, where):
        for src, dst in zip(sources, landing(k)):
            to(src, dst, send, recv, where).start()

    three_bytes = wgu.at[pl.ds(0, 3 * fr), pl.ds(0, hb)]

    def await_block(j, d):
        sem = w_recv.at[turned(a, j) * SIDE + turned(b, d)]
        pltpu.make_async_copy(three_bytes, three_bytes, sem).wait()

    right = (s, v, dp_of(v, a, turned(b, 1)))
    left = (s, v, dp_of(v, a, turned(b, last)))

    def pass_round(j, sources):
        k = dp_of(v, turned(a, j), b)
        recv = w_recv.at[turned(a, j) * SIDE + b]
        three(sources, k, w_send.at[3 + 2 * j], recv, right)
        three(sources, k, w_send.at[4 + 2 * j], recv, left)

    for src, dst in zip(held(a), landing(i)):
        pltpu.make_async_copy(src, dst, own_sem).start()
    for d in range(1, SIDE):
        peer = turned(a, d)
        three(held(peer), i, w_send.at[d - 1], w_recv.at[a * SIDE + b], (s, v, dp_of(v, peer, b)))
    pass_round(0, held(a))

    def to_group(src, block_own, block_other, send, recv):
        for d in range(1, SIDE):
            to(src, gat.at[block_own], send, recv, (s, v, dp_of(v, turned(a, d), b))).start()
        for d in range(SIDE):
            to(src, gat.at[block_other], send, recv, (s, w_other, dp_of(v, a, turned(b, d)))).start()

    def enter(m):
        @pl.when(s == 0)
        def _():
            xin[m] = ent_ref[m]

        @pl.when(s > 0)
        def _():
            pltpu.make_async_copy(xin.at[m], xin.at[m], x_recv.at[m]).wait()

        mine = m * 8 + a * 2 + v
        gat[mine] = rms_scaled(xin[m], gain_ref[...]).astype(jnp.bfloat16)
        to_group(gat.at[mine], mine, m * 8 + b * 2 + v, ag_send.at[m], ag_recv.at[m])

    def branch(m):
        seven = gat.at[pl.ds(0, 7)]
        pltpu.make_async_copy(seven, seven, ag_recv.at[m]).wait()
        rows = gat[pl.ds(pl.multiple_of(m * 8, 8), 8)].reshape(8 * half, width)
        both = jnp.dot(rows, wgu[...], preferred_element_type=jnp.float32)
        gate, up = both[:, :hb], both[:, hb:]
        hid[...] = (gate / (1.0 + jnp.exp(-gate)) * up).astype(jnp.bfloat16)
        out = jnp.dot(hid[...], wdn[...], preferred_element_type=jnp.float32)
        part[pl.ds(pl.multiple_of(m * 8, 8), 8)] = out.astype(jnp.bfloat16).reshape(8, half, width)
        slot = m * 8 + v * SIDE + a
        for d in range(1, SIDE):
            c = turned(a, d)
            for w in (0, 1):
                to(part.at[m * 8 + c * 2 + w], arr.at[slot], rs_send.at[m], rs_recv.at[m],
                   (s, w, dp_of(v, c, b))).start()
        to(part.at[m * 8 + a * 2 + w_other], arr.at[slot], rs_send.at[m], rs_recv.at[m], (s, w_other, i)).start()
        arr[slot] = part[m * 8 + a * 2 + v]

    def leave(m):
        seven = arr.at[pl.ds(0, 7)]
        pltpu.make_async_copy(seven, seven, rs_recv.at[m]).wait()
        total = arr[m * 8].astype(jnp.float32)
        for k in range(1, 8):
            total = total + arr[m * 8 + k].astype(jnp.float32)
        state = xin[m].astype(jnp.float32)
        state = jnp.where(act_ref[m] > 0.0, state + total, state).astype(jnp.bfloat16)

        @pl.when(s < last)
        def _():
            xout[m] = state
            to(xout.at[m], xin.at[m], x_send.at[m], x_recv.at[m], (s + 1, v, i)).start()

        @pl.when(s == last)
        def _():
            fin_ref[m * 2 + v] = rms_scaled(state, fgain_ref[...]).astype(jnp.bfloat16)
            mine = fin_ref.at[m * 2 + v]
            for d in range(1, SIDE):
                for w in (0, 1):
                    to(mine, mine, f_send.at[m], f_recv, (turned(s, d), w, i)).start()
            to(mine, mine, f_send.at[m], f_recv, (s, w_other, i)).start()

    @pl.when(s == 0)
    def _():
        enter(0)
        enter(1)

    for j in range(1, SIDE):
        await_block(j, 0)
        pass_round(j, landing(dp_of(v, turned(a, j), b)))
    for j in range(SIDE):
        d, where = (last, right) if j % 2 == 0 else (1, left)
        await_block(j, d)
        k = dp_of(v, turned(a, j), turned(b, d))
        three(landing(k), k, w_send.at[11 + j], w_recv.at[turned(a, j) * SIDE + turned(b, d)], where)
        await_block(j, SIDE - d)
    for j in range(SIDE):
        await_block(j, 2)
    pltpu.make_async_copy(three_bytes, three_bytes, own_sem).wait()

    @pl.when(s > 0)
    def _():
        enter(0)
        enter(1)

    def step(m, carry):
        branch(m)

        @pl.when(m > 0)
        def _():
            leave(m - 1)

        @pl.when(m + 2 < micro)
        def _():
            enter(m + 2)

        return carry

    lax.fori_loop(0, micro, step, 0)
    leave(micro - 1)

    @pl.when(s < last)
    def _():
        pltpu.make_async_copy(fin_ref, fin_ref, f_recv).wait()

    @pl.when(s == last)
    def _():
        others = fin_ref.at[pl.ds(0, micro)]
        pltpu.make_async_copy(others, others, f_recv).wait()

    for k in range(15):
        pltpu.make_async_copy(three_bytes, three_bytes, w_send.at[k]).wait()

    def drain(m, carry):
        seven, one = gat.at[pl.ds(0, 7)], xout.at[0]
        pltpu.make_async_copy(seven, seven, ag_send.at[m]).wait()
        pltpu.make_async_copy(seven, seven, rs_send.at[m]).wait()

        @pl.when(s < last)
        def _():
            pltpu.make_async_copy(one, one, x_send.at[m]).wait()

        @pl.when(s == last)
        def _():
            pltpu.make_async_copy(seven, seven, f_send.at[m]).wait()

        return carry

    lax.fori_loop(0, micro, drain, 0)


def through_layers(rows, active, gain, final_gain, w_gate, w_up, w_down):
    micro, half, width = rows.shape
    hb = w_gate.shape[1] // SIDE
    vmem, any_space = pl.BlockSpec(memory_space=pltpu.VMEM), pl.BlockSpec(memory_space=pl.ANY)
    dma = pltpu.SemaphoreType.DMA
    bf16 = jnp.bfloat16
    return pl.pallas_call(
        layers_kernel,
        out_shape=jax.ShapeDtypeStruct((2 * micro, half, width), bf16),
        in_specs=[vmem] * 4 + [any_space] * 3,
        out_specs=vmem,
        scratch_shapes=[
            pltpu.VMEM((width, 2 * hb), bf16),
            pltpu.VMEM((hb, width), bf16),
            pltpu.VMEM((micro * 8, half, width), bf16),
            pltpu.VMEM((micro * 8, half, width), bf16),
            pltpu.VMEM((micro * 8, half, width), bf16),
            pltpu.VMEM((micro, half, width), bf16),
            pltpu.VMEM((micro, half, width), bf16),
            pltpu.VMEM((8 * half, hb), bf16),
            dma(()), dma((15,)), dma((SIDE * SIDE,)),
            dma((micro,)), dma((micro,)), dma((micro,)), dma((micro,)),
            dma((micro,)), dma((micro,)), dma((micro,)), dma(()),
        ],
        compiler_params=pltpu.CompilerParams(
            collective_id=0, has_side_effects=True, vmem_limit_bytes=56 * 1024 * 1024
        ),
        name="layers",
    )(rows, active, gain, final_gain, w_gate, w_up, w_down)


def head_kernel(columns, fin_ref, head_ref, label_ref, out_ref, peak, total, picked):
    j = pl.program_id(0)
    tile = head_ref.shape[0]
    lines, rows = peak.shape

    @pl.when(j == 0)
    def _():
        peak[...] = jnp.full_like(peak, -1e30)
        total[...] = jnp.zeros_like(total)
        picked[...] = jnp.zeros_like(picked)

    logits = lax.dot_general(
        head_ref[...], fin_ref[...], (((1,), (1,)), ((), ())), preferred_element_type=jnp.float32
    )
    at = lax.broadcasted_iota(jnp.int32, (tile, rows), 0)
    logits = jnp.where(at < columns - j * tile, logits, -1e30)
    found = jnp.where(at == label_ref[...] - j * tile, logits, 0.0)
    values = logits.reshape(tile // lines, lines, rows)
    old = peak[...]
    new = jnp.maximum(old, jnp.max(values, axis=0))
    summed = total[...] * jnp.exp(old - new) + jnp.sum(jnp.exp(values - new), axis=0)
    found = picked[...] + jnp.sum(found.reshape(values.shape), axis=0)
    peak[...], total[...], picked[...] = new, summed, found

    @pl.when(j == pl.num_programs(0) - 1)
    def _():
        top = jnp.max(new, axis=0, keepdims=True)
        out_ref[0:1, :] = top
        out_ref[1:2, :] = jnp.sum(summed * jnp.exp(new - top), axis=0, keepdims=True)
        out_ref[2:3, :] = jnp.sum(found, axis=0, keepdims=True)
        out_ref[3:8, :] = jnp.zeros((5, rows), jnp.float32)


def head_sums(finals, head_weight, labels, tile=1024):
    rows, width = finals.shape
    columns = head_weight.shape[1]
    return pl.pallas_call(
        functools.partial(head_kernel, columns),
        out_shape=jax.ShapeDtypeStruct((8, rows), jnp.float32),
        grid=(pl.cdiv(columns, tile),),
        in_specs=[
            pl.BlockSpec((rows, width), lambda j: (0, 0)),
            pl.BlockSpec((tile, width), lambda j: (j, 0)),
            pl.BlockSpec((1, rows), lambda j: (0, 0)),
        ],
        out_specs=pl.BlockSpec((8, rows), lambda j: (0, 0)),
        scratch_shapes=[pltpu.VMEM((8, rows), jnp.float32)] * 3,
        compiler_params=pltpu.CompilerParams(vmem_limit_bytes=40 * 1024 * 1024),
        name="head",
    )(finals, head_weight.T, labels)


def losses_kernel(count, sums_ref, loss_ref, mean_ref, shared, totals, own, s_send, s_recv, t_send, t_recv):
    s, v, i = lax.axis_index("section"), lax.axis_index("vocab"), lax.axis_index("dp")
    shards, shares = 8, totals.shape[0]
    barrier = pltpu.get_barrier_semaphore()
    me = s * 2 + v
    for d in range(1, shards):
        k = lax.rem(me + d, shards)
        pl.semaphore_signal(
            barrier, inc=1, device_id=(lax.div(k, 2), lax.rem(k, 2), i), device_id_type=MESH
        )
    for d in range(1, shares):
        pl.semaphore_signal(barrier, inc=1, device_id=(s, v, lax.rem(i + d, shares)), device_id_type=MESH)
    pl.semaphore_wait(barrier, shards + shares - 2)

    for d in range(1, shards):
        k = lax.rem(me + d, shards)
        pltpu.make_async_remote_copy(
            src_ref=sums_ref, dst_ref=shared.at[me], send_sem=s_send, recv_sem=s_recv,
            device_id=(lax.div(k, 2), lax.rem(k, 2), i), device_id_type=MESH,
        ).start()
    shared[me] = sums_ref[...]
    seven = shared.at[pl.ds(0, shards - 1)]
    pltpu.make_async_copy(seven, seven, s_recv).wait()
    everyone = shared[...]
    peaks = everyone[:, 0, :]
    peak = jnp.max(peaks, axis=0, keepdims=True)
    total = jnp.sum(everyone[:, 1, :] * jnp.exp(peaks - peak), axis=0, keepdims=True)
    picked = jnp.sum(everyone[:, 2, :], axis=0, keepdims=True)
    loss = jnp.log(total) + peak - picked
    loss_ref[...] = loss
    own[...] = jnp.broadcast_to(jnp.sum(loss, axis=1, keepdims=True), own.shape)
    for d in range(1, shares):
        pltpu.make_async_remote_copy(
            src_ref=own, dst_ref=totals.at[i], send_sem=t_send, recv_sem=t_recv,
            device_id=(s, v, lax.rem(i + d, shares)), device_id_type=MESH,
        ).start()
    totals[i] = own[...]
    rest = totals.at[pl.ds(0, shares - 1)]
    pltpu.make_async_copy(rest, rest, t_recv).wait()
    mean_ref[...] = jnp.sum(totals[...], axis=0) / count
    pltpu.make_async_copy(seven, seven, s_send).wait()
    pltpu.make_async_copy(rest, rest, t_send).wait()


def losses_of(sums, shares):
    rows = sums.shape[1]
    vmem = pl.BlockSpec(memory_space=pltpu.VMEM)
    dma = pltpu.SemaphoreType.DMA
    return pl.pallas_call(
        functools.partial(losses_kernel, float(rows * shares)),
        out_shape=(jax.ShapeDtypeStruct((1, rows), jnp.float32), jax.ShapeDtypeStruct((8, 128), jnp.float32)),
        in_specs=[vmem],
        out_specs=(vmem, vmem),
        scratch_shapes=[
            pltpu.VMEM((8, 8, rows), jnp.float32),
            pltpu.VMEM((shares, 8, 128), jnp.float32),
            pltpu.VMEM((8, 128), jnp.float32),
            dma(()), dma(()), dma(()), dma(()),
        ],
        compiler_params=pltpu.CompilerParams(collective_id=1, has_side_effects=True),
        name="losses",
    )(sums)


def on_device(entering, depths, targets, norm_gain, w_gate, w_up, w_down, final_gain, head_weight):
    s, v = lax.axis_index("section"), lax.axis_index("vocab")
    micro, _, half, width = entering.shape
    active = jnp.broadcast_to((s < depths).astype(jnp.float32)[:, None, None], (micro, 1, width))
    finals = through_layers(
        entering[:, 0], active, norm_gain, final_gain[None, :], w_gate[0], w_up[0], w_down[0]
    )
    rows = micro * 2 * half
    columns = head_weight.shape[1]
    labels = targets.reshape(1, rows) - (s * 2 + v) * columns
    labels = jnp.where(labels < columns, labels, -1)
    sums = head_sums(finals.reshape(rows, width), head_weight, labels)
    loss, mean = losses_of(sums, lax.axis_size("dp"))
    return loss.reshape(targets.shape), mean[0, 0]


def solution(mesh):
    in_specs = (
        P(None, "dp", "vocab", None),
        P(),
        P(None, "dp", None),
        P("section", None),
        P("section", "dp", "vocab"),
        P("section", "dp", "vocab"),
        P("section", "vocab", "dp"),
        P(),
        P(None, ("section", "vocab")),
    )
    out_specs = (P(None, "dp", None), P())
    return jax.shard_map(
        on_device, mesh=mesh, in_specs=in_specs, out_specs=out_specs, check_vma=False
    )
```

```python
import jax
import jax.numpy as jnp
from jax import lax
from jax.experimental import pallas as pl
from jax.experimental.pallas import tpu as pltpu
from jax.sharding import PartitionSpec as P

EPS = 1e-05
MESH = pl.DeviceIdType.MESH
SIDE = 4


def rms_scaled(values, gain):
    widened = values.astype(jnp.float32)
    return widened * lax.rsqrt(jnp.mean(widened * widened, axis=-1, keepdims=True) + EPS) * gain


def place():
    s, v, i = lax.axis_index("section"), lax.axis_index("vocab"), lax.axis_index("dp")
    z, y = lax.div(i, SIDE), lax.rem(i, SIDE)
    return s, v, i, y + v * (z - y), z + v * (y - z)


def dp_of(v, a, b):
    return SIDE * b + a + v * (SIDE - 1) * (a - b)


def turned(x, d):
    return lax.rem(x + d, SIDE)


def window_kernel(
    depth_ref, ent_ref, gain_ref, fgain_ref, label_ref, wg_ref, wu_ref, wd_ref, head_ref,
    loss_ref, mean_ref,
    wgu, wdn, gat, part, arr, xin, xout, hid, fin, fin_t, head, peak, total, picked, shared, totals,
    own_sem, w_send, w_recv, ag_send, ag_recv, rs_send, rs_recv, x_send, x_recv, f_send, f_recv,
    h_sem, s_send, s_recv, t_send, t_recv,
):
    s, v, i, a, b = place()
    micro, half, width = ent_ref.shape
    hb = hid.shape[1]
    fr = wg_ref.shape[0]
    columns = head_ref.shape[0]
    shares = totals.shape[0]
    w_other = 1 - v
    last = SIDE - 1
    heads = 2 * SIDE

    def to(src, dst, send, recv, where):
        return pltpu.make_async_remote_copy(
            src_ref=src, dst_ref=dst, send_sem=send, recv_sem=recv, device_id=where, device_id_type=MESH
        )

    def await_bytes(ref, sem):
        pltpu.make_async_copy(ref, ref, sem).wait()

    barrier = pltpu.get_barrier_semaphore()

    def greet(where):
        pl.semaphore_signal(barrier, inc=1, device_id=where, device_id_type=MESH)

    for d in range(1, SIDE):
        for w in (0, 1):
            greet((s, w, dp_of(v, turned(a, d), b)))
            greet((s, w, dp_of(v, a, turned(b, d))))
            greet((turned(s, d), w, i))
        for e in range(1, SIDE):
            greet((s, v, dp_of(v, turned(a, d), turned(b, e))))
    greet((s, w_other, i))
    pl.semaphore_wait(barrier, last * (6 + last) + 1)

    def landing(k):
        rows = pl.ds(pl.multiple_of(k * fr, fr), fr)
        return wgu.at[rows, pl.ds(0, hb)], wgu.at[rows, pl.ds(hb, hb)], wdn.at[:, rows]

    def held(k):
        units = pl.ds(pl.multiple_of(k * hb, hb), hb)
        return wg_ref.at[:, units], wu_ref.at[:, units], wd_ref.at[units, :]

    def three(sources, k, send, recv, where):
        for src, dst in zip(sources, landing(k)):
            to(src, dst, send, recv, where).start()

    three_bytes = wgu.at[pl.ds(0, 3 * fr), pl.ds(0, hb)]

    def await_block(j, d):
        await_bytes(three_bytes, w_recv.at[turned(a, j) * SIDE + turned(b, d)])

    right = (s, v, dp_of(v, a, turned(b, 1)))
    left = (s, v, dp_of(v, a, turned(b, last)))

    def pass_round(j, sources):
        k = dp_of(v, turned(a, j), b)
        recv = w_recv.at[turned(a, j) * SIDE + b]
        three(sources, k, w_send.at[3 + 2 * j], recv, right)
        three(sources, k, w_send.at[4 + 2 * j], recv, left)

    for src, dst in zip(held(a), landing(i)):
        pltpu.make_async_copy(src, dst, own_sem).start()
    for d in range(1, SIDE):
        peer = turned(a, d)
        three(held(peer), i, w_send.at[d - 1], w_recv.at[a * SIDE + b], (s, v, dp_of(v, peer, b)))
    pass_round(0, held(a))

    def to_group(src, block_own, block_other, send, recv):
        for d in range(1, SIDE):
            to(src, gat.at[block_own], send, recv, (s, v, dp_of(v, turned(a, d), b))).start()
        for d in range(SIDE):
            to(src, gat.at[block_other], send, recv, (s, w_other, dp_of(v, a, turned(b, d)))).start()

    def enter(m):
        @pl.when(s == 0)
        def _():
            xin[m] = ent_ref[m]

        @pl.when(s > 0)
        def _():
            await_bytes(xin.at[m], x_recv.at[m])

        mine = m * 8 + a * 2 + v
        gat[mine] = rms_scaled(xin[m], gain_ref[...]).astype(jnp.bfloat16)
        to_group(gat.at[mine], mine, m * 8 + b * 2 + v, ag_send.at[m], ag_recv.at[m])

    def branch(m):
        seven = gat.at[pl.ds(0, 7)]
        await_bytes(seven, ag_recv.at[m])
        rows = gat[pl.ds(pl.multiple_of(m * 8, 8), 8)].reshape(8 * half, width)
        both = jnp.dot(rows, wgu[...], preferred_element_type=jnp.float32)
        gate, up = both[:, :hb], both[:, hb:]
        hid[...] = (gate / (1.0 + jnp.exp(-gate)) * up).astype(jnp.bfloat16)
        out = jnp.dot(hid[...], wdn[...], preferred_element_type=jnp.float32)
        part[pl.ds(pl.multiple_of(m * 8, 8), 8)] = out.astype(jnp.bfloat16).reshape(8, half, width)
        slot = m * 8 + v * SIDE + a
        for d in range(1, SIDE):
            c = turned(a, d)
            for w in (0, 1):
                to(part.at[m * 8 + c * 2 + w], arr.at[slot], rs_send.at[m], rs_recv.at[m],
                   (s, w, dp_of(v, c, b))).start()
        to(part.at[m * 8 + a * 2 + w_other], arr.at[slot], rs_send.at[m], rs_recv.at[m], (s, w_other, i)).start()
        arr[slot] = part[m * 8 + a * 2 + v]

    def leave(m):
        seven = arr.at[pl.ds(0, 7)]
        await_bytes(seven, rs_recv.at[m])
        added = arr[m * 8].astype(jnp.float32)
        for k in range(1, 8):
            added = added + arr[m * 8 + k].astype(jnp.float32)
        state = xin[m].astype(jnp.float32)
        active = jnp.full(state.shape, depth_ref[m], jnp.int32) > s
        state = jnp.where(active, state + added, state).astype(jnp.bfloat16)

        @pl.when(s < last)
        def _():
            xout[m] = state
            to(xout.at[m], xin.at[m], x_send.at[m], x_recv.at[m], (s + 1, v, i)).start()

        @pl.when(s == last)
        def _():
            fin[m * 2 + v] = rms_scaled(state, fgain_ref[...]).astype(jnp.bfloat16)
            mine = fin.at[m * 2 + v]
            for d in range(1, SIDE):
                for w in (0, 1):
                    to(mine, mine, f_send.at[m], f_recv, (turned(s, d), w, i)).start()
            to(mine, mine, f_send.at[m], f_recv, (s, w_other, i)).start()

    @pl.when(s == 0)
    def _():
        enter(0)
        enter(1)

    pltpu.make_async_copy(head_ref, head, h_sem).start()

    for j in range(1, SIDE):
        await_block(j, 0)
        pass_round(j, landing(dp_of(v, turned(a, j), b)))
    for j in range(SIDE):
        d, where = (last, right) if j % 2 == 0 else (1, left)
        await_block(j, d)
        k = dp_of(v, turned(a, j), turned(b, d))
        three(landing(k), k, w_send.at[11 + j], w_recv.at[turned(a, j) * SIDE + turned(b, d)], where)
        await_block(j, SIDE - d)
    for j in range(SIDE):
        await_block(j, 2)
    await_bytes(three_bytes, own_sem)

    @pl.when(s > 0)
    def _():
        enter(0)
        enter(1)

    def step(m, carry):
        branch(m)

        @pl.when(m > 0)
        def _():
            leave(m - 1)

        @pl.when(m + 2 < micro)
        def _():
            enter(m + 2)

        return carry

    lax.fori_loop(0, micro, step, 0)
    leave(micro - 1)

    await_bytes(head, h_sem)

    @pl.when(s < last)
    def _():
        await_bytes(fin, f_recv)

    @pl.when(s == last)
    def _():
        await_bytes(fin.at[pl.ds(0, micro)], f_recv)

    lines, positions = peak.shape
    fin_t[...] = jnp.transpose(fin[...].reshape(positions, width))
    peak[...] = jnp.full_like(peak, -1e30)
    total[...] = jnp.zeros_like(total)
    picked[...] = jnp.zeros_like(picked)
    labels = label_ref[...]

    def tile_sums(start, size):
        logits = jnp.dot(head[pl.ds(start, size), :], fin_t[...], preferred_element_type=jnp.float32)
        at = lax.broadcasted_iota(jnp.int32, (size, positions), 0)
        found = jnp.where(at == labels - start, logits, 0.0)
        values = logits.reshape(size // lines, lines, positions)
        old = peak[...]
        new = jnp.maximum(old, jnp.max(values, axis=0))
        total[...] = total[...] * jnp.exp(old - new) + jnp.sum(jnp.exp(values - new), axis=0)
        picked[...] = picked[...] + jnp.sum(found.reshape(values.shape), axis=0)
        peak[...] = new

    tile = TILE
    full = columns // tile

    def one_tile(j, carry):
        tile_sums(pl.multiple_of(j * tile, tile), tile)
        return carry

    lax.fori_loop(0, full, one_tile, 0)
    if columns % tile:
        tile_sums(full * tile, columns % tile)

    me = s * 2 + v
    new = peak[...]
    top = jnp.max(new, axis=0, keepdims=True)
    shared[me, 0:1, :] = top
    shared[me, 1:2, :] = jnp.sum(total[...] * jnp.exp(new - top), axis=0, keepdims=True)
    shared[me, 2:3, :] = jnp.sum(picked[...], axis=0, keepdims=True)
    shared[me, 3:8, :] = jnp.zeros((5, positions), jnp.float32)
    mine = shared.at[me]
    for d in range(SIDE):
        for w in (0, 1):
            if d:
                to(mine, mine, s_send, s_recv, (turned(s, d), w, i)).start()
    to(mine, mine, s_send, s_recv, (s, w_other, i)).start()
    seven = shared.at[pl.ds(0, heads - 1)]
    await_bytes(seven, s_recv)
    everyone = shared[...]
    peaks = everyone[:, 0, :]
    top = jnp.max(peaks, axis=0, keepdims=True)
    summed = jnp.sum(everyone[:, 1, :] * jnp.exp(peaks - top), axis=0, keepdims=True)
    loss = jnp.log(summed) + top - jnp.sum(everyone[:, 2, :], axis=0, keepdims=True)
    totals[i] = jnp.broadcast_to(jnp.sum(loss, axis=1, keepdims=True), totals.shape[1:])
    for d in range(1, shares):
        to(totals.at[i], totals.at[i], t_send, t_recv, (s, v, lax.rem(i + d, shares))).start()
    for m in range(micro):
        loss_ref[m] = loss[:, 2 * half * m : 2 * half * (m + 1)]

    for k in range(15):
        await_bytes(three_bytes, w_send.at[k])

    def drain(m, carry):
        await_bytes(gat.at[pl.ds(0, heads - 1)], ag_send.at[m])
        await_bytes(gat.at[pl.ds(0, heads - 1)], rs_send.at[m])

        @pl.when(s < last)
        def _():
            await_bytes(xout.at[0], x_send.at[m])

        @pl.when(s == last)
        def _():
            await_bytes(gat.at[pl.ds(0, heads - 1)], f_send.at[m])

        return carry

    lax.fori_loop(0, micro, drain, 0)
    await_bytes(seven, s_send)
    rest = totals.at[pl.ds(0, shares - 1)]
    await_bytes(rest, t_recv)
    mean_ref[...] = jnp.sum(totals[...], axis=0)[0:1, 0:1] / float(shares * positions)
    await_bytes(rest, t_send)


TILE = 1024


def on_device(entering, depths, targets, norm_gain, w_gate, w_up, w_down, final_gain, head_weight):
    s, v, shares = lax.axis_index("section"), lax.axis_index("vocab"), lax.axis_size("dp")
    micro, _, half, width = entering.shape
    columns = head_weight.shape[1]
    hb = w_gate.shape[2] // SIDE
    positions = micro * 2 * half
    labels = targets.reshape(1, positions) - (s * 2 + v) * columns
    vmem, any_space = pl.BlockSpec(memory_space=pltpu.VMEM), pl.BlockSpec(memory_space=pl.ANY)
    dma, held = pltpu.SemaphoreType.DMA, pltpu.VMEM
    bf16, f32 = jnp.bfloat16, jnp.float32
    rows = (half, width)
    return pl.pallas_call(
        window_kernel,
        out_shape=(
            jax.ShapeDtypeStruct((micro, 1, 2 * half), f32),
            jax.ShapeDtypeStruct((1, 1), f32),
        ),
        in_specs=[pl.BlockSpec(memory_space=pltpu.SMEM)] + [vmem] * 4 + [any_space] * 4,
        out_specs=(vmem, vmem),
        scratch_shapes=[
            held((width, 2 * hb), bf16),
            held((hb, width), bf16),
            held((micro * 2 * SIDE, *rows), bf16),
            held((micro * 2 * SIDE, *rows), bf16),
            held((micro * 2 * SIDE, *rows), bf16),
            held((micro, *rows), bf16),
            held((micro, *rows), bf16),
            held((2 * SIDE * half, hb), bf16),
            held((micro * 2, *rows), bf16),
            held((width, positions), bf16),
            held((columns, width), bf16),
            held((8, positions), f32), held((8, positions), f32), held((8, positions), f32),
            held((2 * SIDE, 8, positions), f32),
            held((shares, 8, 128), f32),
            dma(()), dma((15,)), dma((SIDE * SIDE,)),
            dma((micro,)), dma((micro,)), dma((micro,)), dma((micro,)),
            dma((micro,)), dma((micro,)), dma((micro,)), dma(()),
            dma(()), dma(()), dma(()), dma(()), dma(()),
        ],
        compiler_params=pltpu.CompilerParams(
            collective_id=0, has_side_effects=True, vmem_limit_bytes=67043328
        ),
        name="window",
    )(depths, entering[:, 0], norm_gain, final_gain[None, :], labels, w_gate[0], w_up[0], w_down[0], head_weight.T)


def per_device(*args):
    loss, mean = on_device(*args)
    return loss, mean.reshape(())


def solution(mesh):
    in_specs = (
        P(None, "dp", "vocab", None),
        P(),
        P(None, "dp", None),
        P("section", None),
        P("section", "dp", "vocab"),
        P("section", "dp", "vocab"),
        P("section", "vocab", "dp"),
        P(),
        P(None, ("section", "vocab")),
    )
    out_specs = (P(None, "dp", None), P())
    return jax.shard_map(
        per_device, mesh=mesh, in_specs=in_specs, out_specs=out_specs, check_vma=False
    )
```

```python
import jax
import jax.numpy as jnp
from jax import lax
from jax.experimental import pallas as pl
from jax.experimental.pallas import tpu as pltpu
from jax.sharding import PartitionSpec as P

EPS = 1e-05
MESH = pl.DeviceIdType.MESH
SIDE = 4


DETOURS = ((0, 3, 0), (1, 1, 1))


def rms_scaled(values, gain):
    widened = values.astype(jnp.float32)
    return widened * lax.rsqrt(jnp.mean(widened * widened, axis=-1, keepdims=True) + EPS) * gain


def place():
    s, v, i = lax.axis_index("section"), lax.axis_index("vocab"), lax.axis_index("dp")
    z, y = lax.div(i, SIDE), lax.rem(i, SIDE)
    return s, v, i, y + v * (z - y), z + v * (y - z)


def dp_of(v, a, b):
    return SIDE * b + a + v * (SIDE - 1) * (a - b)


def turned(x, d):
    return lax.rem(x + d, SIDE)


def window_kernel(
    depth_ref, ent_ref, gain_ref, fgain_ref, label_ref, wg_ref, wu_ref, wd_ref, head_ref,
    loss_ref, mean_ref,
    wgu, wdn, gat, part, arr, xin, xout, hid, fin, fin_t, head, peak, total, picked, shared, totals,
    own_sem, w_send, w_recv, ag_send, ag_recv, rs_send, rs_recv, x_send, x_recv, f_send, f_recv,
    st_send, st_recv, h_sem, s_send, s_recv, t_send, t_recv,
):
    s, v, i, a, b = place()
    micro, half, width = ent_ref.shape
    hb = hid.shape[1]
    fr = wg_ref.shape[0]
    columns = head_ref.shape[0]
    shares = totals.shape[0]
    w_other = 1 - v
    last = SIDE - 1
    heads = 2 * SIDE

    def to(src, dst, send, recv, where):
        return pltpu.make_async_remote_copy(
            src_ref=src, dst_ref=dst, send_sem=send, recv_sem=recv, device_id=where, device_id_type=MESH
        )

    def await_bytes(ref, sem):
        pltpu.make_async_copy(ref, ref, sem).wait()

    barrier = pltpu.get_barrier_semaphore()

    def greet(where):
        pl.semaphore_signal(barrier, inc=1, device_id=where, device_id_type=MESH)

    for d in range(1, SIDE):
        for w in (0, 1):
            greet((s, w, dp_of(v, turned(a, d), b)))
            greet((s, w, dp_of(v, a, turned(b, d))))
            greet((turned(s, d), w, i))
        for e in range(1, SIDE):
            greet((s, v, dp_of(v, turned(a, d), turned(b, e))))
    for d in (1, last):
        greet((turned(s, d), v, dp_of(v, a, turned(b, 2))))
    greet((s, w_other, i))
    pl.semaphore_wait(barrier, last * (6 + last) + 3)

    def landing(k):
        rows = pl.ds(pl.multiple_of(k * fr, fr), fr)
        return wgu.at[rows, pl.ds(0, hb)], wgu.at[rows, pl.ds(hb, hb)], wdn.at[:, rows]

    def held(k):
        units = pl.ds(pl.multiple_of(k * hb, hb), hb)
        return wg_ref.at[:, units], wu_ref.at[:, units], wd_ref.at[units, :]

    def three(sources, k, send, recv, where):
        for src, dst in zip(sources, landing(k)):
            to(src, dst, send, recv, where).start()

    three_bytes = wgu.at[pl.ds(0, 3 * fr), pl.ds(0, hb)]

    def await_block(j, d):
        await_bytes(three_bytes, w_recv.at[turned(a, j) * SIDE + turned(b, d)])

    right = (s, v, dp_of(v, a, turned(b, 1)))
    left = (s, v, dp_of(v, a, turned(b, last)))

    def pass_round(j, sources):
        k = dp_of(v, turned(a, j), b)
        recv = w_recv.at[turned(a, j) * SIDE + b]
        three(sources, k, w_send.at[3 + 2 * j], recv, right)
        three(sources, k, w_send.at[4 + 2 * j], recv, left)

    for src, dst in zip(held(a), landing(i)):
        pltpu.make_async_copy(src, dst, own_sem).start()
    for d in range(1, SIDE):
        peer = turned(a, d)
        three(held(peer), i, w_send.at[d - 1], w_recv.at[a * SIDE + b], (s, v, dp_of(v, peer, b)))
    pass_round(0, held(a))

    def stage(n):
        top = n * (fr + hb)
        return (
            head.at[pl.ds(top, fr), pl.ds(0, hb)],
            head.at[pl.ds(top, fr), pl.ds(hb, hb)],
            head.at[pl.ds(top + fr, hb), pl.ds(0, fr)],
        )

    def detour(j, sources):
        for n, (turn, helper, _) in enumerate(DETOURS):
            if turn == j:
                @pl.when(s == 0)
                def _():
                    where = (helper, v, dp_of(v, a, turned(b, 2)))
                    for src, dst in zip(sources, stage(n)):
                        to(src, dst, w_send.at[11 + j], st_recv.at[n], where).start()

    def help_on(j):
        for n, (turn, helper, after) in enumerate(DETOURS):
            if after == j:
                @pl.when(s == helper)
                def _():
                    await_bytes(three_bytes, st_recv.at[n])
                    k = dp_of(v, turned(a, turn), turned(b, 2))
                    recv = w_recv.at[turned(a, turn) * SIDE + turned(b, 2)]
                    three(stage(n), k, st_send.at[n], recv, (0, v, i))

    detour(0, held(a))

    def to_group(src, block_own, block_other, send, recv):
        for d in range(1, SIDE):
            to(src, gat.at[block_own], send, recv, (s, v, dp_of(v, turned(a, d), b))).start()
        for d in range(SIDE):
            to(src, gat.at[block_other], send, recv, (s, w_other, dp_of(v, a, turned(b, d)))).start()

    def enter(m):
        @pl.when(s == 0)
        def _():
            xin[m] = ent_ref[m]

        @pl.when(s > 0)
        def _():
            await_bytes(xin.at[m], x_recv.at[m])

        mine = m * 8 + a * 2 + v
        gat[mine] = rms_scaled(xin[m], gain_ref[...]).astype(jnp.bfloat16)
        to_group(gat.at[mine], mine, m * 8 + b * 2 + v, ag_send.at[m], ag_recv.at[m])

    def branch(m):
        seven = gat.at[pl.ds(0, 7)]
        await_bytes(seven, ag_recv.at[m])
        rows = gat[pl.ds(pl.multiple_of(m * 8, 8), 8)].reshape(8 * half, width)
        both = jnp.dot(rows, wgu[...], preferred_element_type=jnp.float32)
        gate, up = both[:, :hb], both[:, hb:]
        hid[...] = (gate / (1.0 + jnp.exp(-gate)) * up).astype(jnp.bfloat16)
        out = jnp.dot(hid[...], wdn[...], preferred_element_type=jnp.float32)
        part[pl.ds(pl.multiple_of(m * 8, 8), 8)] = out.astype(jnp.bfloat16).reshape(8, half, width)
        slot = m * 8 + v * SIDE + a
        for d in range(1, SIDE):
            c = turned(a, d)
            for w in (0, 1):
                to(part.at[m * 8 + c * 2 + w], arr.at[slot], rs_send.at[m], rs_recv.at[m],
                   (s, w, dp_of(v, c, b))).start()
        to(part.at[m * 8 + a * 2 + w_other], arr.at[slot], rs_send.at[m], rs_recv.at[m], (s, w_other, i)).start()
        arr[slot] = part[m * 8 + a * 2 + v]

    def leave(m):
        seven = arr.at[pl.ds(0, 7)]
        await_bytes(seven, rs_recv.at[m])
        added = arr[m * 8].astype(jnp.float32)
        for k in range(1, 8):
            added = added + arr[m * 8 + k].astype(jnp.float32)
        state = xin[m].astype(jnp.float32)
        active = jnp.full(state.shape, depth_ref[m], jnp.int32) > s
        state = jnp.where(active, state + added, state).astype(jnp.bfloat16)

        @pl.when(s < last)
        def _():
            xout[m] = state
            to(xout.at[m], xin.at[m], x_send.at[m], x_recv.at[m], (s + 1, v, i)).start()

        @pl.when(s == last)
        def _():
            fin[m * 2 + v] = rms_scaled(state, fgain_ref[...]).astype(jnp.bfloat16)
            mine = fin.at[m * 2 + v]
            for d in range(1, SIDE):
                for w in (0, 1):
                    to(mine, mine, f_send.at[m], f_recv, (turned(s, d), w, i)).start()
            to(mine, mine, f_send.at[m], f_recv, (s, w_other, i)).start()

    @pl.when(s == 0)
    def _():
        enter(0)
        enter(1)

    for j in range(1, SIDE):
        await_block(j, 0)
        block = landing(dp_of(v, turned(a, j), b))
        pass_round(j, block)
        detour(j, block)
    help_on(-1)
    for j in range(SIDE):
        d, where = (last, right) if j % 2 == 0 else (1, left)
        await_block(j, d)
        k = dp_of(v, turned(a, j), turned(b, d))

        def forward():
            three(landing(k), k, w_send.at[11 + j], w_recv.at[turned(a, j) * SIDE + turned(b, d)], where)

        if any(turn == j for turn, _, _ in DETOURS):
            pl.when(s != 0)(forward)
        else:
            forward()
        await_block(j, SIDE - d)
        help_on(j)
    for j in range(SIDE):
        await_block(j, 2)
    await_bytes(three_bytes, own_sem)

    for n, (_, helper, _) in enumerate(DETOURS):
        @pl.when(s == helper)
        def _():
            await_bytes(three_bytes, st_send.at[n])

    pltpu.make_async_copy(head_ref, head, h_sem).start()

    @pl.when(s > 0)
    def _():
        enter(0)
        enter(1)

    def step(m, carry):
        branch(m)

        @pl.when(m > 0)
        def _():
            leave(m - 1)

        @pl.when(m + 2 < micro)
        def _():
            enter(m + 2)

        return carry

    lax.fori_loop(0, micro, step, 0)
    leave(micro - 1)

    await_bytes(head, h_sem)

    @pl.when(s < last)
    def _():
        await_bytes(fin, f_recv)

    @pl.when(s == last)
    def _():
        await_bytes(fin.at[pl.ds(0, micro)], f_recv)

    lines, positions = peak.shape
    fin_t[...] = jnp.transpose(fin[...].reshape(positions, width))
    peak[...] = jnp.full_like(peak, -1e30)
    total[...] = jnp.zeros_like(total)
    picked[...] = jnp.zeros_like(picked)
    labels = label_ref[...]

    def tile_sums(start, size):
        logits = jnp.dot(head[pl.ds(start, size), :], fin_t[...], preferred_element_type=jnp.float32)
        at = lax.broadcasted_iota(jnp.int32, (size, positions), 0)
        found = jnp.where(at == labels - start, logits, 0.0)
        values = logits.reshape(size // lines, lines, positions)
        old = peak[...]
        new = jnp.maximum(old, jnp.max(values, axis=0))
        total[...] = total[...] * jnp.exp(old - new) + jnp.sum(jnp.exp(values - new), axis=0)
        picked[...] = picked[...] + jnp.sum(found.reshape(values.shape), axis=0)
        peak[...] = new

    tile = TILE
    full = columns // tile

    def some_tiles(j, carry):
        for k in range(3):
            tile_sums(pl.multiple_of((j * 3 + k) * tile, tile), tile)
        return carry

    lax.fori_loop(0, full // 3, some_tiles, 0)
    if columns % tile:
        tile_sums(full * tile, columns % tile)

    me = s * 2 + v
    new = peak[...]
    top = jnp.max(new, axis=0, keepdims=True)
    shared[me, 0:1, :] = top
    shared[me, 1:2, :] = jnp.sum(total[...] * jnp.exp(new - top), axis=0, keepdims=True)
    shared[me, 2:3, :] = jnp.sum(picked[...], axis=0, keepdims=True)
    shared[me, 3:8, :] = jnp.zeros((5, positions), jnp.float32)
    mine = shared.at[me]
    for d in range(SIDE):
        for w in (0, 1):
            if d:
                to(mine, mine, s_send, s_recv, (turned(s, d), w, i)).start()
    to(mine, mine, s_send, s_recv, (s, w_other, i)).start()
    seven = shared.at[pl.ds(0, heads - 1)]
    await_bytes(seven, s_recv)
    everyone = shared[...]
    peaks = everyone[:, 0, :]
    top = jnp.max(peaks, axis=0, keepdims=True)
    summed = jnp.sum(everyone[:, 1, :] * jnp.exp(peaks - top), axis=0, keepdims=True)
    loss = jnp.log(summed) + top - jnp.sum(everyone[:, 2, :], axis=0, keepdims=True)
    totals[i] = jnp.broadcast_to(jnp.sum(loss, axis=1, keepdims=True), totals.shape[1:])
    for d in range(1, shares):
        to(totals.at[i], totals.at[i], t_send, t_recv, (s, v, lax.rem(i + d, shares))).start()
    for m in range(micro):
        loss_ref[m] = loss[:, 2 * half * m : 2 * half * (m + 1)]

    for k in range(15):
        await_bytes(three_bytes, w_send.at[k])

    def drain(m, carry):
        await_bytes(gat.at[pl.ds(0, heads - 1)], ag_send.at[m])
        await_bytes(gat.at[pl.ds(0, heads - 1)], rs_send.at[m])

        @pl.when(s < last)
        def _():
            await_bytes(xout.at[0], x_send.at[m])

        @pl.when(s == last)
        def _():
            await_bytes(gat.at[pl.ds(0, heads - 1)], f_send.at[m])

        return carry

    lax.fori_loop(0, micro, drain, 0)
    await_bytes(seven, s_send)
    rest = totals.at[pl.ds(0, shares - 1)]
    await_bytes(rest, t_recv)
    mean_ref[...] = jnp.sum(totals[...], axis=0)[0:1, 0:1] / float(shares * positions)
    await_bytes(rest, t_send)


TILE = 512


def on_device(entering, depths, targets, norm_gain, w_gate, w_up, w_down, final_gain, head_weight):
    s, v, shares = lax.axis_index("section"), lax.axis_index("vocab"), lax.axis_size("dp")
    micro, _, half, width = entering.shape
    columns = head_weight.shape[1]
    hb = w_gate.shape[2] // SIDE
    positions = micro * 2 * half
    labels = targets.reshape(1, positions) - (s * 2 + v) * columns
    vmem, any_space = pl.BlockSpec(memory_space=pltpu.VMEM), pl.BlockSpec(memory_space=pl.ANY)
    dma, held = pltpu.SemaphoreType.DMA, pltpu.VMEM
    bf16, f32 = jnp.bfloat16, jnp.float32
    rows = (half, width)
    return pl.pallas_call(
        window_kernel,
        out_shape=(
            jax.ShapeDtypeStruct((micro, 1, 2 * half), f32),
            jax.ShapeDtypeStruct((1, 1), f32),
        ),
        in_specs=[pl.BlockSpec(memory_space=pltpu.SMEM)] + [vmem] * 4 + [any_space] * 4,
        out_specs=(vmem, vmem),
        scratch_shapes=[
            held((width, 2 * hb), bf16),
            held((hb, width), bf16),
            held((micro * 2 * SIDE, *rows), bf16),
            held((micro * 2 * SIDE, *rows), bf16),
            held((micro * 2 * SIDE, *rows), bf16),
            held((micro, *rows), bf16),
            held((micro, *rows), bf16),
            held((2 * SIDE * half, hb), bf16),
            held((micro * 2, *rows), bf16),
            held((width, positions), bf16),
            held((columns, width), bf16),
            held((8, positions), f32), held((8, positions), f32), held((8, positions), f32),
            held((2 * SIDE, 8, positions), f32),
            held((shares, 8, 128), f32),
            dma(()), dma((15,)), dma((SIDE * SIDE,)),
            dma((micro,)), dma((micro,)), dma((micro,)), dma((micro,)),
            dma((micro,)), dma((micro,)), dma((micro,)), dma(()),
            dma((len(DETOURS),)), dma((len(DETOURS),)), dma(()), dma(()), dma(()), dma(()), dma(()),
        ],
        compiler_params=pltpu.CompilerParams(
            collective_id=0, has_side_effects=True, vmem_limit_bytes=67043328
        ),
        name="window",
    )(depths, entering[:, 0], norm_gain, final_gain[None, :], labels, w_gate[0], w_up[0], w_down[0], head_weight.T)


def per_device(*args):
    loss, mean = on_device(*args)
    return loss, mean.reshape(())


def solution(mesh):
    in_specs = (
        P(None, "dp", "vocab", None),
        P(),
        P(None, "dp", None),
        P("section", None),
        P("section", "dp", "vocab"),
        P("section", "dp", "vocab"),
        P("section", "vocab", "dp"),
        P(),
        P(None, ("section", "vocab")),
    )
    out_specs = (P(None, "dp", None), P())
    return jax.shard_map(
        per_device, mesh=mesh, in_specs=in_specs, out_specs=out_specs, check_vma=False
    )
```

```python
import jax
import jax.numpy as jnp
from jax import lax
from jax.experimental import pallas as pl
from jax.experimental.pallas import tpu as pltpu
from jax.sharding import PartitionSpec as P

EPS = 1e-05
MESH = pl.DeviceIdType.MESH
SIDE = 4


DETOURS = ((0, 3, 0), (1, 1, 1))


def rms_scaled(values, gain):
    widened = values.astype(jnp.float32)
    return widened * lax.rsqrt(jnp.mean(widened * widened, axis=-1, keepdims=True) + EPS) * gain


def place():
    s, v, i = lax.axis_index("section"), lax.axis_index("vocab"), lax.axis_index("dp")
    z, y = lax.div(i, SIDE), lax.rem(i, SIDE)
    return s, v, i, y + v * (z - y), z + v * (y - z)


def dp_of(v, a, b):
    return SIDE * b + a + v * (SIDE - 1) * (a - b)


def turned(x, d):
    return lax.rem(x + d, SIDE)


def window_kernel(
    depth_ref, ent_ref, gain_ref, fgain_ref, label_ref, wg_ref, wu_ref, wd_ref, head_ref,
    loss_ref, mean_ref,
    wgu, wdn, gat, part, arr, xin, xout, hid, fin, fin_t, head, label, peak, total, picked, shared, totals,
    own_sem, w_send, w_recv, ag_send, ag_recv, rs_send, rs_recv, x_send, x_recv, f_send, f_recv,
    st_send, st_recv, e_sem, h_sem, s_send, s_recv, t_send, t_recv,
):
    s, v, i, a, b = place()
    micro, half, width = ent_ref.shape
    hb = hid.shape[1]
    fr = wg_ref.shape[0]
    columns = head_ref.shape[0]
    shares = totals.shape[0]
    w_other = 1 - v
    last = SIDE - 1
    heads = 2 * SIDE

    def to(src, dst, send, recv, where):
        return pltpu.make_async_remote_copy(
            src_ref=src, dst_ref=dst, send_sem=send, recv_sem=recv, device_id=where, device_id_type=MESH
        )

    def await_bytes(ref, sem):
        pltpu.make_async_copy(ref, ref, sem).wait()

    @pl.when(s == 0)
    def _():
        pltpu.make_async_copy(ent_ref, xin, e_sem).start()

    barrier = pltpu.get_barrier_semaphore()

    def greet(where):
        pl.semaphore_signal(barrier, inc=1, device_id=where, device_id_type=MESH)

    for d in range(1, SIDE):
        for w in (0, 1):
            greet((s, w, dp_of(v, turned(a, d), b)))
            greet((s, w, dp_of(v, a, turned(b, d))))
            greet((turned(s, d), w, i))
        for e in range(1, SIDE):
            greet((s, v, dp_of(v, turned(a, d), turned(b, e))))
    for d in (1, last):
        greet((turned(s, d), v, dp_of(v, a, turned(b, 2))))
    greet((s, w_other, i))
    pl.semaphore_wait(barrier, last * (6 + last) + 3)

    def landing(k):
        rows = pl.ds(pl.multiple_of(k * fr, fr), fr)
        return wgu.at[rows, pl.ds(0, hb)], wgu.at[rows, pl.ds(hb, hb)], wdn.at[:, rows]

    def held(k):
        units = pl.ds(pl.multiple_of(k * hb, hb), hb)
        return wg_ref.at[:, units], wu_ref.at[:, units], wd_ref.at[units, :]

    def three(sources, k, send, recv, where):
        for src, dst in zip(sources, landing(k)):
            to(src, dst, send, recv, where).start()

    three_bytes = wgu.at[pl.ds(0, 3 * fr), pl.ds(0, hb)]

    def await_block(j, d):
        await_bytes(three_bytes, w_recv.at[turned(a, j) * SIDE + turned(b, d)])

    right = (s, v, dp_of(v, a, turned(b, 1)))
    left = (s, v, dp_of(v, a, turned(b, last)))

    def pass_round(j, sources):
        k = dp_of(v, turned(a, j), b)
        recv = w_recv.at[turned(a, j) * SIDE + b]
        three(sources, k, w_send.at[3 + 2 * j], recv, right)
        three(sources, k, w_send.at[4 + 2 * j], recv, left)

    for src, dst in zip(held(a), landing(i)):
        pltpu.make_async_copy(src, dst, own_sem).start()
    for d in range(1, SIDE):
        peer = turned(a, d)
        three(held(peer), i, w_send.at[d - 1], w_recv.at[a * SIDE + b], (s, v, dp_of(v, peer, b)))
    pass_round(0, held(a))

    def stage(n):
        top = n * (fr + hb)
        return (
            head.at[pl.ds(top, fr), pl.ds(0, hb)],
            head.at[pl.ds(top, fr), pl.ds(hb, hb)],
            head.at[pl.ds(top + fr, hb), pl.ds(0, fr)],
        )

    def detour(j, sources):
        for n, (turn, helper, _) in enumerate(DETOURS):
            if turn == j:
                @pl.when(s == 0)
                def _():
                    where = (helper, v, dp_of(v, a, turned(b, 2)))
                    for src, dst in zip(sources, stage(n)):
                        to(src, dst, w_send.at[11 + j], st_recv.at[n], where).start()

    def help_on(j):
        for n, (turn, helper, after) in enumerate(DETOURS):
            if after == j:
                @pl.when(s == helper)
                def _():
                    await_bytes(three_bytes, st_recv.at[n])
                    k = dp_of(v, turned(a, turn), turned(b, 2))
                    recv = w_recv.at[turned(a, turn) * SIDE + turned(b, 2)]
                    three(stage(n), k, st_send.at[n], recv, (0, v, i))

    detour(0, held(a))

    def to_group(src, block_own, block_other, send, recv):
        for d in range(1, SIDE):
            to(src, gat.at[block_own], send, recv, (s, v, dp_of(v, turned(a, d), b))).start()
        for d in range(SIDE):
            to(src, gat.at[block_other], send, recv, (s, w_other, dp_of(v, a, turned(b, d)))).start()

    def enter(m):
        @pl.when(s > 0)
        def _():
            await_bytes(xin.at[m], x_recv.at[m])

        mine = m * 8 + a * 2 + v
        gat[mine] = rms_scaled(xin[m], gain_ref[...]).astype(jnp.bfloat16)
        to_group(gat.at[mine], mine, m * 8 + b * 2 + v, ag_send.at[m], ag_recv.at[m])

    def branch(m):
        seven = gat.at[pl.ds(0, 7)]
        await_bytes(seven, ag_recv.at[m])
        rows = gat[pl.ds(pl.multiple_of(m * 8, 8), 8)].reshape(8 * half, width)
        both = jnp.dot(rows, wgu[...], preferred_element_type=jnp.float32)
        gate, up = both[:, :hb], both[:, hb:]
        hid[...] = (gate / (1.0 + jnp.exp(-gate)) * up).astype(jnp.bfloat16)
        out = jnp.dot(hid[...], wdn[...], preferred_element_type=jnp.float32)
        part[pl.ds(pl.multiple_of(m * 8, 8), 8)] = out.astype(jnp.bfloat16).reshape(8, half, width)
        slot = m * 8 + v * SIDE + a
        for d in range(1, SIDE):
            c = turned(a, d)
            for w in (0, 1):
                to(part.at[m * 8 + c * 2 + w], arr.at[slot], rs_send.at[m], rs_recv.at[m],
                   (s, w, dp_of(v, c, b))).start()
        to(part.at[m * 8 + a * 2 + w_other], arr.at[slot], rs_send.at[m], rs_recv.at[m], (s, w_other, i)).start()
        arr[slot] = part[m * 8 + a * 2 + v]

    def leave(m):
        seven = arr.at[pl.ds(0, 7)]
        await_bytes(seven, rs_recv.at[m])
        added = arr[m * 8].astype(jnp.float32)
        for k in range(1, 8):
            added = added + arr[m * 8 + k].astype(jnp.float32)
        state = xin[m].astype(jnp.float32)
        active = jnp.full(state.shape, depth_ref[m], jnp.int32) > s
        state = jnp.where(active, state + added, state).astype(jnp.bfloat16)

        @pl.when(s < last)
        def _():
            xout[m] = state
            to(xout.at[m], xin.at[m], x_send.at[m], x_recv.at[m], (s + 1, v, i)).start()

        @pl.when(s == last)
        def _():
            fin[m * 2 + v] = rms_scaled(state, fgain_ref[...]).astype(jnp.bfloat16)
            mine = fin.at[m * 2 + v]
            for d in range(1, SIDE):
                for w in (0, 1):
                    to(mine, mine, f_send.at[m], f_recv, (turned(s, d), w, i)).start()
            to(mine, mine, f_send.at[m], f_recv, (s, w_other, i)).start()

    @pl.when(s == 0)
    def _():
        await_bytes(xin, e_sem)
        enter(0)
        enter(1)

    for j in range(1, SIDE):
        await_block(j, 0)
        block = landing(dp_of(v, turned(a, j), b))
        pass_round(j, block)
        detour(j, block)
    help_on(-1)
    for j in range(SIDE):
        d, where = (last, right) if j % 2 == 0 else (1, left)
        await_block(j, d)
        k = dp_of(v, turned(a, j), turned(b, d))

        def forward():
            three(landing(k), k, w_send.at[11 + j], w_recv.at[turned(a, j) * SIDE + turned(b, d)], where)

        if any(turn == j for turn, _, _ in DETOURS):
            pl.when(s != 0)(forward)
        else:
            forward()
        await_block(j, SIDE - d)
        help_on(j)
    for j in range(SIDE):
        await_block(j, 2)
    await_bytes(three_bytes, own_sem)

    for n, (_, helper, _) in enumerate(DETOURS):
        @pl.when(s == helper)
        def _():
            await_bytes(three_bytes, st_send.at[n])

    pltpu.make_async_copy(head_ref, head, h_sem).start()

    @pl.when(s > 0)
    def _():
        enter(0)
        enter(1)

    def step(m, carry):
        branch(m)

        @pl.when(m > 0)
        def _():
            leave(m - 1)

        @pl.when(m + 2 < micro)
        def _():
            enter(m + 2)

        return carry

    lax.fori_loop(0, micro, step, 0)
    leave(micro - 1)

    await_bytes(head, h_sem)

    @pl.when(s < last)
    def _():
        await_bytes(fin, f_recv)

    @pl.when(s == last)
    def _():
        await_bytes(fin.at[pl.ds(0, micro)], f_recv)

    lines, positions = peak.shape
    fin_t[...] = jnp.transpose(fin[...].reshape(positions, width))
    peak[...] = jnp.full_like(peak, -1e30)
    total[...] = jnp.zeros_like(total)
    picked[...] = jnp.zeros_like(picked)
    for m in range(micro):
        label[:, 2 * half * m : 2 * half * (m + 1)] = label_ref[m]
    labels = label[...] - (s * 2 + v) * columns

    def tile_sums(start, size):
        logits = jnp.dot(head[pl.ds(start, size), :], fin_t[...], preferred_element_type=jnp.float32)
        at = lax.broadcasted_iota(jnp.int32, (size, positions), 0)
        found = jnp.where(at == labels - start, logits, 0.0)
        values = logits.reshape(size // lines, lines, positions)
        old = peak[...]
        new = jnp.maximum(old, jnp.max(values, axis=0))
        total[...] = total[...] * jnp.exp(old - new) + jnp.sum(jnp.exp(values - new), axis=0)
        picked[...] = picked[...] + jnp.sum(found.reshape(values.shape), axis=0)
        peak[...] = new

    tile = TILE
    full = columns // tile

    def some_tiles(j, carry):
        for k in range(3):
            tile_sums(pl.multiple_of((j * 3 + k) * tile, tile), tile)
        return carry

    lax.fori_loop(0, full // 3, some_tiles, 0)
    if columns % tile:
        tile_sums(full * tile, columns % tile)

    me = s * 2 + v
    new = peak[...]
    top = jnp.max(new, axis=0, keepdims=True)
    shared[me, 0:1, :] = top
    shared[me, 1:2, :] = jnp.sum(total[...] * jnp.exp(new - top), axis=0, keepdims=True)
    shared[me, 2:3, :] = jnp.sum(picked[...], axis=0, keepdims=True)
    shared[me, 3:8, :] = jnp.zeros((5, positions), jnp.float32)
    mine = shared.at[me]
    for d in range(SIDE):
        for w in (0, 1):
            if d:
                to(mine, mine, s_send, s_recv, (turned(s, d), w, i)).start()
    to(mine, mine, s_send, s_recv, (s, w_other, i)).start()
    seven = shared.at[pl.ds(0, heads - 1)]
    await_bytes(seven, s_recv)
    everyone = shared[...]
    peaks = everyone[:, 0, :]
    top = jnp.max(peaks, axis=0, keepdims=True)
    summed = jnp.sum(everyone[:, 1, :] * jnp.exp(peaks - top), axis=0, keepdims=True)
    loss = jnp.log(summed) + top - jnp.sum(everyone[:, 2, :], axis=0, keepdims=True)
    totals[i] = jnp.broadcast_to(jnp.sum(loss, axis=1, keepdims=True), totals.shape[1:])
    for d in range(1, shares):
        to(totals.at[i], totals.at[i], t_send, t_recv, (s, v, lax.rem(i + d, shares))).start()
    for m in range(micro):
        loss_ref[m] = loss[:, 2 * half * m : 2 * half * (m + 1)]

    for k in range(15):
        await_bytes(three_bytes, w_send.at[k])

    def drain(m, carry):
        await_bytes(gat.at[pl.ds(0, heads - 1)], ag_send.at[m])
        await_bytes(gat.at[pl.ds(0, heads - 1)], rs_send.at[m])

        @pl.when(s < last)
        def _():
            await_bytes(xout.at[0], x_send.at[m])

        @pl.when(s == last)
        def _():
            await_bytes(gat.at[pl.ds(0, heads - 1)], f_send.at[m])

        return carry

    lax.fori_loop(0, micro, drain, 0)
    await_bytes(seven, s_send)
    rest = totals.at[pl.ds(0, shares - 1)]
    await_bytes(rest, t_recv)
    mean_ref[...] = jnp.sum(totals[...], axis=0)[0:1, 0:1] / float(shares * positions)
    await_bytes(rest, t_send)


TILE = 512


def on_device(entering, depths, targets, norm_gain, w_gate, w_up, w_down, final_gain, head_weight):
    shares = lax.axis_size("dp")
    micro, _, half, width = entering.shape
    columns = head_weight.shape[1]
    hb = w_gate.shape[2] // SIDE
    positions = micro * 2 * half
    vmem, any_space = pl.BlockSpec(memory_space=pltpu.VMEM), pl.BlockSpec(memory_space=pl.ANY)
    dma, held = pltpu.SemaphoreType.DMA, pltpu.VMEM
    bf16, f32 = jnp.bfloat16, jnp.float32
    rows = (half, width)
    return pl.pallas_call(
        window_kernel,
        out_shape=(
            jax.ShapeDtypeStruct((micro, 1, 2 * half), f32),
            jax.ShapeDtypeStruct((1, 1), f32),
        ),
        in_specs=[pl.BlockSpec(memory_space=pltpu.SMEM), any_space] + [vmem] * 3 + [any_space] * 4,
        out_specs=(vmem, vmem),
        scratch_shapes=[
            held((width, 2 * hb), bf16),
            held((hb, width), bf16),
            held((micro * 2 * SIDE, *rows), bf16),
            held((micro * 2 * SIDE, *rows), bf16),
            held((micro * 2 * SIDE, *rows), bf16),
            held((micro, *rows), bf16),
            held((micro, *rows), bf16),
            held((2 * SIDE * half, hb), bf16),
            held((micro * 2, *rows), bf16),
            held((width, positions), bf16),
            held((columns, width), bf16),
            held((1, positions), jnp.int32),
            held((8, positions), f32), held((8, positions), f32), held((8, positions), f32),
            held((2 * SIDE, 8, positions), f32),
            held((shares, 8, 128), f32),
            dma(()), dma((15,)), dma((SIDE * SIDE,)),
            dma((micro,)), dma((micro,)), dma((micro,)), dma((micro,)),
            dma((micro,)), dma((micro,)), dma((micro,)), dma(()),
            dma((len(DETOURS),)), dma((len(DETOURS),)), dma(()), dma(()), dma(()), dma(()), dma(()), dma(()),
        ],
        compiler_params=pltpu.CompilerParams(
            collective_id=0, has_side_effects=True, vmem_limit_bytes=67043328
        ),
        name="window",
    )(depths, entering[:, 0], norm_gain, final_gain[None, :], targets, w_gate[0], w_up[0], w_down[0], head_weight.T)


def per_device(*args):
    loss, mean = on_device(*args)
    return loss, mean.reshape(())


def solution(mesh):
    in_specs = (
        P(None, "dp", "vocab", None),
        P(),
        P(None, "dp", None),
        P("section", None),
        P("section", "dp", "vocab"),
        P("section", "dp", "vocab"),
        P("section", "vocab", "dp"),
        P(),
        P(None, ("section", "vocab")),
    )
    out_specs = (P(None, "dp", None), P())
    return jax.shard_map(
        per_device, mesh=mesh, in_specs=in_specs, out_specs=out_specs, check_vma=False
    )
```
